32 devices in a mesh: freq: 4 (over y, x), bond: 8 (over z, core).
Axes of the slice: x: 2, y: 2, z: 4, core: 2. Of those that a mesh axis runs over, the one named last changes fastest.
Arguments:
- gamma: bfloat16 [2, 8, 32, 384, 384], P(None, 'freq', 'bond'), may hold values from -1 to 1
- green: float32 [2, 8, 32, 256], P(None, 'freq', 'bond'), may hold values from -6 to 6
- single: float32 [2, 8, 32, 256], P(None, 'freq', 'bond'), may hold values from -6 to 6
- bond_site: int32 [384], replicated, may hold values from 0 to 255
- causal_mask: int32 [8, 3, 3], P('freq'), may hold values 0 or 1
- site_perm: int32 [384], replicated, may hold values from 0 to 383, each once
Outputs:
- p_vertex: bfloat16 [2, 8, 384, 32, 384], P(None, 'freq', 'bond')
The draws below stay inside these ranges and needn't reach their ends.
Inputs may be any that keep to these rules, and one draw needn't show every extreme that they name: `bond_site`: each of the 384 bond-Keldysh indices names one site. `causal_mask`: 1 keeps a causality block of 128 x 128 entries, 0 removes it. `site_perm`: a permutation of the 384 column indices.
All inputs are finite; a program needn't handle non-finite values.
Results may differ from the reference program's by a relative error of at most 0.0049.
Values may be sent and summed in bfloat16 or wider, within the bound.
A program may use at most 128 MiB of HBM per device.

```python
import math
import jax
import jax.numpy as jnp
from jax import lax

M = 384
KBLK = 3
SITES = 256
BLK = 128
W = 8
SEGS = 32


def with_ends(values, rng, low, top_value):
    longest = values.shape.index(max(values.shape))
    spots = []
    for shift in (0, 1):
        where = [jax.random.randint(jax.random.fold_in(rng, axis), (), 0, length) for axis, length in enumerate(values.shape)]
        where[longest] = (where[longest] + shift) % values.shape[longest]
        spots.append(tuple(where))
    return values.at[spots[0]].set(low).at[spots[1]].set(top_value)


def block_levels(own_key, shape, split, smallest, high):
    factor_of = 1.0
    for dim, blocks in split:
        heights = jax.random.uniform(jax.random.fold_in(jax.random.fold_in(own_key, 6), dim), (blocks,), jnp.float32, smallest / len(split), high / len(split))
        factor_of = factor_of * jnp.repeat(jnp.exp(heights), shape[dim] // blocks).reshape((-1,) + (1,) * (len(shape) - 1 - dim))
    return factor_of


def bell_draw(stream_key, shape, scale, reach, pieces=(), kind=jnp.bfloat16):
    level = block_levels(stream_key, shape, pieces, -0.22, 0.18) if pieces else 1.0
    entries = jax.random.normal(stream_key, shape, jnp.float32) * scale * level
    return jnp.minimum(jnp.maximum(entries, -reach), reach).astype(kind)


def setup_inputs(seed: int = 0) -> dict:
    keys = jax.random.split(jax.random.key(seed), 7)
    gamma = bell_draw(keys[0], (2, W, SEGS, M, M), 0.125, 1.0, ((1, 4), (2, 8)))
    green = bell_draw(keys[1], (2, W, SEGS, SITES), 1.0, 6.0, ((1, 4), (2, 8)), jnp.float32)
    single = bell_draw(keys[2], (2, W, SEGS, SITES), 1.0, 6.0, ((1, 4), (2, 8)), jnp.float32)
    bond_site = with_ends(jax.random.randint(keys[3], (M,), 0, SITES), jax.random.fold_in(keys[3], 1), 0, SITES - 1).astype(jnp.int32)
    causal_mask = with_ends((jax.random.randint(keys[4], (W, KBLK, KBLK), 0, 3) < 2).astype(jnp.int32), jax.random.fold_in(keys[4], 1), 0, 1)
    site_perm = jax.random.permutation(keys[5], M).astype(jnp.int32)
    return dict(gamma=gamma, green=green, single=single, bond_site=bond_site, causal_mask=causal_mask, site_perm=site_perm)


def times_complex(first_real, first_imag, second_real, second_imag):
    return (first_real * second_real - first_imag * second_imag, first_real * second_imag + first_imag * second_real)

def make_bubble(green, single, bond_site):
    green_bond = jnp.take(green, bond_site, axis=3)
    single_bond = jnp.take(single, bond_site, axis=3)
    count = green.shape[1]
    steps_all = jnp.arange(count, dtype=jnp.int32)
    shifts = (steps_all[None, :] + steps_all[:, None]) % count
    green_moved = jnp.take(green_bond, shifts, axis=1)
    single_moved = jnp.take(single_bond, shifts, axis=1)
    first = times_complex(green_bond[0][None], green_bond[1][None], single_moved[0], single_moved[1])
    second = times_complex(single_bond[0][None], single_bond[1][None], green_moved[0], green_moved[1])
    factor = 1.0 / math.sqrt(count)
    bubble_real = lax.optimization_barrier(jnp.sum(first[0] + second[0], axis=1)) * factor
    bubble_imag = lax.optimization_barrier(jnp.sum(first[1] + second[1], axis=1)) * factor
    return jnp.stack([bubble_real, bubble_imag])

def flow_one(items):
    gamma_here, bubble_here, mask_here, site_perm = items
    gamma_real = gamma_here[0].astype(jnp.float32)
    gamma_imag = gamma_here[1].astype(jnp.float32)
    bubble_real = bubble_here[0][:, None, :]
    bubble_imag = bubble_here[1][:, None, :]
    left_real = (gamma_real * bubble_real - gamma_imag * bubble_imag).astype(jnp.bfloat16)
    left_imag = (gamma_real * bubble_imag + gamma_imag * bubble_real).astype(jnp.bfloat16)
    left_real = lax.optimization_barrier(left_real).astype(jnp.float32)
    left_imag = lax.optimization_barrier(left_imag).astype(jnp.float32)
    highest = lax.Precision.HIGHEST
    flow_real = jnp.einsum('srk,skc->rsc', left_real, gamma_real, precision=highest) - jnp.einsum('srk,skc->rsc', left_imag, gamma_imag, precision=highest)
    flow_imag = jnp.einsum('srk,skc->rsc', left_real, gamma_imag, precision=highest) + jnp.einsum('srk,skc->rsc', left_imag, gamma_real, precision=highest)
    spread = jnp.repeat(jnp.repeat(mask_here, BLK, axis=0), BLK, axis=1).astype(jnp.float32)
    flow_real = flow_real * spread[:, None, :]
    flow_imag = flow_imag * spread[:, None, :]
    rounded = jnp.stack([flow_real, flow_imag]).astype(jnp.bfloat16)
    return jnp.take(rounded, site_perm, axis=3)

def reference(gamma, green, single, bond_site, causal_mask, site_perm):
    bubble = make_bubble(green, single, bond_site)
    count = gamma.shape[1]
    perms = jnp.broadcast_to(site_perm[None, :], (count, site_perm.shape[0]))
    result = lax.map(flow_one, (jnp.moveaxis(gamma, 1, 0), jnp.moveaxis(bubble, 1, 0), causal_mask, perms))
    return jnp.moveaxis(result, 0, 1)
```

```python
import functools
import math

import jax
import jax.numpy as jnp
from jax import lax
from jax.experimental import pallas as pl
from jax.experimental.pallas import tpu as pltpu
from jax.sharding import PartitionSpec as P

LANES = 128


def partner(index, step, count):
    if count & (count - 1):
        return lax.rem(index + step, count)
    found = 0
    bit = 1
    while bit < count:
        found = found + lax.rem(index // bit + (step // bit) % 2, 2) * bit
        bit *= 2
    return found


def origin(index, step, count):
    if count & (count - 1):
        return lax.rem(index + count - step, count)
    return partner(index, step, count)


def times_complex(a, b, c, d):
    return a * c - b * d, a * d + b * c


def kernel(nf, nb, gamma, green, single, bond, mask, perm, out,
           all_green, all_single, bubble, masks, shuffle, send, land, stage,
           recv_g, recv_s, send_g, send_s, send_sem, recv_sem, own_sem):
    _, local, sites_here, order, _ = gamma.shape
    sites = green.shape[-1]
    blocks = mask.shape[-1]
    width = order // blocks
    rows = order // nb
    count = local * nf
    seg = nb * sites_here
    items = local * sites_here
    f = lax.axis_index("freq")
    b = lax.axis_index("bond")

    barrier = pltpu.get_barrier_semaphore()
    for step in range(1, nf):
        pl.semaphore_signal(barrier, inc=1, device_id={"freq": lax.rem(f + step, nf)},
                            device_id_type=pl.DeviceIdType.MESH)
    for step in range(1, nb):
        pl.semaphore_signal(barrier, inc=1, device_id={"bond": partner(b, step, nb)},
                            device_id_type=pl.DeviceIdType.MESH)
    pl.semaphore_wait(barrier, nf - 1 + nb - 1)

    def greens(step):
        to = lax.rem(f + step, nf)
        pair = []
        for source, landing, ss, rs in ((green, all_green, send_g, recv_g),
                                        (single, all_single, send_s, recv_s)):
            pair.append(pltpu.make_async_remote_copy(
                src_ref=source, dst_ref=landing.at[f], send_sem=ss.at[step],
                recv_sem=rs.at[step], device_id={"freq": to},
                device_id_type=pl.DeviceIdType.MESH))
        return pair

    for step in range(1, nf):
        for copy in greens(step):
            copy.start()
    all_green[f] = green[...]
    all_single[f] = single[...]

    pick = (lax.broadcasted_iota(jnp.int32, (sites, order), 0) == bond[...]).astype(jnp.float32)
    shuffle[...] = (lax.broadcasted_iota(jnp.int32, (order, order), 0) == perm[...]).astype(
        jnp.float32).astype(jnp.bfloat16)
    for w in range(local):
        for i in range(blocks):
            for j in range(blocks):
                masks[w, i * width:(i + 1) * width, j * width:(j + 1) * width] = jnp.full(
                    (width, width), mask[w, i, j].astype(jnp.float32), jnp.float32)

    for step in range(1, nf):
        for copy in greens(step):
            copy.wait()

    factor = 1.0 / math.sqrt(count)
    for w in range(local):
        real = jnp.zeros((sites_here, sites), jnp.float32)
        imag = jnp.zeros((sites_here, sites), jnp.float32)
        for v in range(count):
            moved = lax.rem(f * local + (w + v), count)
            far, near = moved // local, lax.rem(moved, local)
            g = [all_green[v // local, part, v % local] for part in range(2)]
            s = [all_single[v // local, part, v % local] for part in range(2)]
            gm = [all_green[far, part, near] for part in range(2)]
            sm = [all_single[far, part, near] for part in range(2)]
            first = times_complex(g[0], g[1], sm[0], sm[1])
            second = times_complex(s[0], s[1], gm[0], gm[1])
            real = real + (first[0] + second[0])
            imag = imag + (first[1] + second[1])
        for part, value in enumerate((real, imag)):
            bubble[part, w] = jnp.dot(value * factor, pick, precision=lax.Precision.HIGHEST,
                                      preferred_element_type=jnp.float32)

    def own(i):
        return pltpu.make_async_copy(send.at[i, b], land.at[i, b], own_sem.at[i])

    def outgoing(i, step):
        to = partner(b, step, nb)
        return pltpu.make_async_remote_copy(
            src_ref=send.at[i, to], dst_ref=land.at[i, b], send_sem=send_sem.at[i, step],
            recv_sem=recv_sem.at[i, step], device_id={"bond": to},
            device_id_type=pl.DeviceIdType.MESH)

    def compute(i, carry):
        w, s = i // sites_here, lax.rem(i, sites_here)
        gr, gi = gamma[0, w, s], gamma[1, w, s]
        br, bi = bubble[0, w, pl.ds(s, 1), :], bubble[1, w, pl.ds(s, 1), :]
        grf, gif = gr.astype(jnp.float32), gi.astype(jnp.float32)
        lr = (grf * br - gif * bi).astype(jnp.bfloat16)
        li = (grf * bi + gif * br).astype(jnp.bfloat16)
        left = jnp.concatenate([lr, li], axis=1)
        fr = jnp.dot(left, jnp.concatenate([gr, -gi], axis=0), preferred_element_type=jnp.float32)
        fi = jnp.dot(left, jnp.concatenate([gi, gr], axis=0), preferred_element_type=jnp.float32)
        for part, flow in enumerate((fr, fi)):
            kept = (flow * masks[w]).astype(jnp.bfloat16)
            moved = jnp.dot(kept, shuffle[...], preferred_element_type=jnp.float32).astype(jnp.bfloat16)
            for d in range(nb):
                send[i, d, part] = moved[d * rows:(d + 1) * rows]
        for step in range(nb - 1, 0, -1):
            outgoing(i, step).start()
        own(i).start()
        return carry

    lax.fori_loop(0, items, compute, 0)

    def arrange(i, src):
        w, s = i // sites_here, lax.rem(i, sites_here)
        for part in range(2):
            block = land[i, src, part].astype(jnp.float32)
            for c in range(order // LANES):
                stage[w, part, c, pl.ds(src * sites_here + s, rows, stride=seg), :] = (
                    block[:, c * LANES:(c + 1) * LANES])

    def receive(i, carry):
        own(i).wait()
        arrange(i, b)
        for step in range(1, nb):
            copy = outgoing(i, step)
            copy.wait_recv()
            arrange(i, origin(b, step, nb))
        return carry

    for w in range(local):
        lax.fori_loop(w * sites_here, (w + 1) * sites_here, receive, 0)
        for part in range(2):
            for c in range(order // LANES):
                out[part, w, :, :, c * LANES:(c + 1) * LANES] = (
                    stage[w, part, c].reshape(rows, seg, LANES).astype(jnp.bfloat16))

    def drain(i, carry):
        for step in range(1, nb):
            outgoing(i, step).wait_send()
        return carry

    lax.fori_loop(0, items, drain, 0)


def body(nf, nb, gamma, green, single, bond_site, causal_mask, site_perm):
    _, local, sites_here, order, _ = gamma.shape
    sites = green.shape[-1]
    rows = order // nb
    seg = nb * sites_here
    items = local * sites_here
    vmem = pl.BlockSpec(memory_space=pltpu.VMEM)
    dma = pltpu.SemaphoreType.DMA
    return pl.pallas_call(
        functools.partial(kernel, nf, nb),
        out_shape=jax.ShapeDtypeStruct((2, local, rows, seg, order), jnp.bfloat16),
        in_specs=[vmem, vmem, vmem, vmem, pl.BlockSpec(memory_space=pltpu.SMEM), vmem],
        out_specs=vmem,
        scratch_shapes=[
            pltpu.VMEM((nf, 2, local, sites_here, sites), jnp.float32),
            pltpu.VMEM((nf, 2, local, sites_here, sites), jnp.float32),
            pltpu.VMEM((2, local, sites_here, order), jnp.float32),
            pltpu.VMEM((local, order, order), jnp.float32),
            pltpu.VMEM((order, order), jnp.bfloat16),
            pltpu.VMEM((items, nb, 2, rows, order), jnp.bfloat16),
            pltpu.VMEM((items, nb, 2, rows, order), jnp.bfloat16),
            pltpu.VMEM((local, 2, order // LANES, rows * seg, LANES), jnp.float32),
            dma((nf,)), dma((nf,)), dma((nf,)), dma((nf,)),
            dma((items, nb)), dma((items, nb)), dma((items,)),
        ],
        compiler_params=pltpu.CompilerParams(
            collective_id=0, has_side_effects=True, vmem_limit_bytes=60 * 1024 * 1024),
        name="flow_exchange",
    )(gamma, green, single, bond_site[None, :], causal_mask, site_perm[None, :])


def solution(mesh):
    in_specs = (
        P(None, "freq", "bond", None, None),
        P(None, "freq", "bond", None),
        P(None, "freq", "bond", None),
        P(),
        P("freq", None, None),
        P(),
    )
    out_specs = P(None, "freq", "bond", None, None)
    run = functools.partial(body, mesh.shape["freq"], mesh.shape["bond"])
    return jax.shard_map(run, mesh=mesh, in_specs=in_specs, out_specs=out_specs, check_vma=False)
```

```python
import functools
import math

import jax
import jax.numpy as jnp
from jax import lax
from jax.experimental import pallas as pl
from jax.experimental.pallas import tpu as pltpu
from jax.sharding import PartitionSpec as P

LANES = 128
WINDOW = 2


def partner(index, step, count):
    if count & (count - 1):
        return lax.rem(index + step, count)
    found = 0
    bit = 1
    while bit < count:
        found = found + lax.rem(index // bit + (step // bit) % 2, 2) * bit
        bit *= 2
    return found


def origin(index, step, count):
    if count & (count - 1):
        return lax.rem(index + count - step, count)
    return partner(index, step, count)


def times_complex(a, b, c, d):
    return a * c - b * d, a * d + b * c


def kernel(nf, nb, gamma, green, single, bond, mask, perm, out,
           all_green, all_single, bubble, masks, shuffle, send, land, stage,
           recv_g, recv_s, send_g, send_s, send_sem, recv_sem, own_sem):
    _, local, sites_here, order, _ = gamma.shape
    sites = green.shape[-1]
    blocks = mask.shape[-1]
    width = order // blocks
    rows = order // nb
    count = local * nf
    seg = nb * sites_here
    items = local * sites_here
    f = lax.axis_index("freq")
    b = lax.axis_index("bond")

    barrier = pltpu.get_barrier_semaphore()
    for step in range(1, nf):
        pl.semaphore_signal(barrier, inc=1, device_id={"freq": lax.rem(f + step, nf)},
                            device_id_type=pl.DeviceIdType.MESH)
    for step in range(1, nb):
        pl.semaphore_signal(barrier, inc=1, device_id={"bond": partner(b, step, nb)},
                            device_id_type=pl.DeviceIdType.MESH)
    pl.semaphore_wait(barrier, nf - 1 + nb - 1)

    def greens(step):
        to = lax.rem(f + step, nf)
        pair = []
        for source, landing, ss, rs in ((green, all_green, send_g, recv_g),
                                        (single, all_single, send_s, recv_s)):
            pair.append(pltpu.make_async_remote_copy(
                src_ref=source, dst_ref=landing.at[f], send_sem=ss.at[step],
                recv_sem=rs.at[step], device_id={"freq": to},
                device_id_type=pl.DeviceIdType.MESH))
        return pair

    for step in range(1, nf):
        for copy in greens(step):
            copy.start()
    all_green[f] = green[...]
    all_single[f] = single[...]

    pick = (lax.broadcasted_iota(jnp.int32, (sites, order), 0) == bond[...][None, :]).astype(jnp.float32)
    shuffle[...] = (lax.broadcasted_iota(jnp.int32, (order, order), 0) == perm[...][None, :]).astype(
        jnp.float32).astype(jnp.bfloat16)
    for w in range(local):
        for i in range(blocks):
            for j in range(blocks):
                masks[w, i * width:(i + 1) * width, j * width:(j + 1) * width] = jnp.full(
                    (width, width), mask[i, w, j].astype(jnp.float32), jnp.float32)

    for step in range(1, nf):
        for copy in greens(step):
            copy.wait()

    factor = 1.0 / math.sqrt(count)
    for w in range(local):
        real = jnp.zeros((sites_here, sites), jnp.float32)
        imag = jnp.zeros((sites_here, sites), jnp.float32)
        for v in range(count):
            moved = lax.rem(f * local + (w + v), count)
            far, near = moved // local, lax.rem(moved, local)
            g = [all_green[v // local, part, v % local] for part in range(2)]
            s = [all_single[v // local, part, v % local] for part in range(2)]
            gm = [all_green[far, part, near] for part in range(2)]
            sm = [all_single[far, part, near] for part in range(2)]
            first = times_complex(g[0], g[1], sm[0], sm[1])
            second = times_complex(s[0], s[1], gm[0], gm[1])
            real = real + (first[0] + second[0])
            imag = imag + (first[1] + second[1])
        for part, value in enumerate((real, imag)):
            bubble[part, w] = jnp.dot(value * factor, pick, precision=lax.Precision.HIGHEST,
                                      preferred_element_type=jnp.float32)

    def own(i):
        return pltpu.make_async_copy(send.at[i, b], land.at[i, b], own_sem.at[i])

    def outgoing(i, step):
        to = partner(b, step, nb)
        return pltpu.make_async_remote_copy(
            src_ref=send.at[i, to], dst_ref=land.at[i, b], send_sem=send_sem.at[i, step],
            recv_sem=recv_sem.at[i, step], device_id={"bond": to},
            device_id_type=pl.DeviceIdType.MESH)

    def compute(i, carry):
        w, s = i // sites_here, lax.rem(i, sites_here)
        gr, gi = gamma[0, w, s], gamma[1, w, s]
        br, bi = bubble[0, w, pl.ds(s, 1), :], bubble[1, w, pl.ds(s, 1), :]
        grf, gif = gr.astype(jnp.float32), gi.astype(jnp.float32)
        lr = (grf * br - gif * bi).astype(jnp.bfloat16)
        li = (grf * bi + gif * br).astype(jnp.bfloat16)
        left = jnp.concatenate([lr, li], axis=1)
        fr = jnp.dot(left, jnp.concatenate([gr, -gi], axis=0), preferred_element_type=jnp.float32)
        fi = jnp.dot(left, jnp.concatenate([gi, gr], axis=0), preferred_element_type=jnp.float32)
        for part, flow in enumerate((fr, fi)):
            kept = (flow * masks[w]).astype(jnp.bfloat16)
            moved = jnp.dot(kept, shuffle[...], preferred_element_type=jnp.float32).astype(jnp.bfloat16)
            for d in range(nb):
                send[i, d, part] = moved[d * rows:(d + 1) * rows]

        @pl.when(i >= WINDOW)
        def _():
            receive(i - WINDOW)

        for step in range(nb - 1, 0, -1):
            outgoing(i, step).start()
        own(i).start()
        return carry

    def arrange(i, src):
        w, s = i // sites_here, lax.rem(i, sites_here)
        for part in range(2):
            block = land[i, src, part].astype(jnp.float32)
            for c in range(order // LANES):
                stage[w, part, c, pl.ds(src * sites_here + s, rows, stride=seg), :] = (
                    block[:, c * LANES:(c + 1) * LANES])

    def receive(i):
        own(i).wait()
        arrange(i, b)
        for step in range(1, nb):
            copy = outgoing(i, step)
            copy.wait_recv()
            arrange(i, origin(b, step, nb))

    def receive_last(i, carry):
        receive(i)
        return carry

    lax.fori_loop(0, items, compute, 0)
    lax.fori_loop(items - WINDOW, items, receive_last, 0)
    for w in range(local):
        for part in range(2):
            for c in range(order // LANES):
                out[part, w, :, :, c * LANES:(c + 1) * LANES] = (
                    stage[w, part, c].reshape(rows, seg, LANES).astype(jnp.bfloat16))

    def drain(i, carry):
        for step in range(1, nb):
            outgoing(i, step).wait_send()
        return carry

    lax.fori_loop(0, items, drain, 0)


def body(nf, nb, gamma, green, single, bond_site, causal_mask, site_perm):
    _, local, sites_here, order, _ = gamma.shape
    sites = green.shape[-1]
    rows = order // nb
    seg = nb * sites_here
    items = local * sites_here
    vmem = pl.BlockSpec(memory_space=pltpu.VMEM)
    dma = pltpu.SemaphoreType.DMA
    return pl.pallas_call(
        functools.partial(kernel, nf, nb),
        out_shape=jax.ShapeDtypeStruct((2, local, rows, seg, order), jnp.bfloat16),
        in_specs=[vmem, vmem, vmem, vmem, pl.BlockSpec(memory_space=pltpu.SMEM), vmem],
        out_specs=vmem,
        scratch_shapes=[
            pltpu.VMEM((nf, 2, local, sites_here, sites), jnp.float32),
            pltpu.VMEM((nf, 2, local, sites_here, sites), jnp.float32),
            pltpu.VMEM((2, local, sites_here, order), jnp.float32),
            pltpu.VMEM((local, order, order), jnp.float32),
            pltpu.VMEM((order, order), jnp.bfloat16),
            pltpu.VMEM((items, nb, 2, rows, order), jnp.bfloat16),
            pltpu.VMEM((items, nb, 2, rows, order), jnp.bfloat16),
            pltpu.VMEM((local, 2, order // LANES, rows * seg, LANES), jnp.float32),
            dma((nf,)), dma((nf,)), dma((nf,)), dma((nf,)),
            dma((items, nb)), dma((items, nb)), dma((items,)),
        ],
        compiler_params=pltpu.CompilerParams(
            collective_id=0, has_side_effects=True, vmem_limit_bytes=60 * 1024 * 1024),
        name="flow_exchange",
    )(gamma, green, single, bond_site, causal_mask.transpose(1, 0, 2), site_perm)


def solution(mesh):
    in_specs = (
        P(None, "freq", "bond", None, None),
        P(None, "freq", "bond", None),
        P(None, "freq", "bond", None),
        P(),
        P("freq", None, None),
        P(),
    )
    out_specs = P(None, "freq", "bond", None, None)
    run = functools.partial(body, mesh.shape["freq"], mesh.shape["bond"])
    return jax.shard_map(run, mesh=mesh, in_specs=in_specs, out_specs=out_specs, check_vma=False)
```

```python
import functools
import math

import jax
import jax.numpy as jnp
from jax import lax
from jax.experimental import pallas as pl
from jax.experimental.pallas import tpu as pltpu
from jax.sharding import PartitionSpec as P

LANES = 128
WINDOW = 2
VMEM_BYTES = 67_043_328


def partner(index, step, count):
    if count & (count - 1):
        return lax.rem(index + step, count)
    found = 0
    bit = 1
    while bit < count:
        found = found + lax.rem(index // bit + (step // bit) % 2, 2) * bit
        bit *= 2
    return found


def origin(index, step, count):
    if count & (count - 1):
        return lax.rem(index + count - step, count)
    return partner(index, step, count)


def times_complex(a, b, c, d):
    return a * c - b * d, a * d + b * c


def kernel(nf, nb, gamma_hbm, green, single, bond, mask, perm, out,
           gamma, gamma_sem, all_green, all_single, bubble, masks, shuffle, send, land, stage,
           recv_g, recv_s, send_g, send_s, send_sem, recv_sem, own_sem):
    _, local, sites_here, order, _ = gamma_hbm.shape
    sites = green.shape[-1]
    blocks = mask.shape[-1]
    width = order // blocks
    rows = order // nb
    count = local * nf
    seg = nb * sites_here
    items = local * sites_here
    f = lax.axis_index("freq")
    b = lax.axis_index("bond")

    def fetch(i):
        w, s = i // sites_here, lax.rem(i, sites_here)
        return pltpu.make_async_copy(gamma_hbm.at[:, w, s], gamma.at[i], gamma_sem.at[i])

    def fetch_start(i, carry):
        fetch(i).start()
        return carry

    barrier = pltpu.get_barrier_semaphore()
    for step in range(1, nf):
        pl.semaphore_signal(barrier, inc=1, device_id={"freq": lax.rem(f + step, nf)},
                            device_id_type=pl.DeviceIdType.MESH)
    for step in range(1, nb):
        pl.semaphore_signal(barrier, inc=1, device_id={"bond": partner(b, step, nb)},
                            device_id_type=pl.DeviceIdType.MESH)
    lax.fori_loop(0, items, fetch_start, 0)

    pick = (lax.broadcasted_iota(jnp.int32, (sites, order), 0) == bond[...][None, :]).astype(jnp.float32)
    shuffle[...] = (lax.broadcasted_iota(jnp.int32, (order, order), 0) == perm[...][None, :]).astype(
        jnp.float32).astype(jnp.bfloat16)
    for w in range(local):
        for i in range(blocks):
            for j in range(blocks):
                masks[w, i * width:(i + 1) * width, j * width:(j + 1) * width] = jnp.full(
                    (width, width), mask[i, w, j].astype(jnp.float32), jnp.float32)

    pl.semaphore_wait(barrier, nf - 1 + nb - 1)

    def greens(step):
        to = lax.rem(f + step, nf)
        pair = []
        for source, landing, ss, rs in ((green, all_green, send_g, recv_g),
                                        (single, all_single, send_s, recv_s)):
            pair.append(pltpu.make_async_remote_copy(
                src_ref=source, dst_ref=landing.at[f], send_sem=ss.at[step],
                recv_sem=rs.at[step], device_id={"freq": to},
                device_id_type=pl.DeviceIdType.MESH))
        return pair

    for step in range(1, nf):
        for copy in greens(step):
            copy.start()
    all_green[f] = green[...]
    all_single[f] = single[...]

    for step in range(1, nf):
        for copy in greens(step):
            copy.wait()

    factor = 1.0 / math.sqrt(count)
    for w in range(local):
        real = jnp.zeros((sites_here, sites), jnp.float32)
        imag = jnp.zeros((sites_here, sites), jnp.float32)
        for v in range(count):
            moved = lax.rem(f * local + (w + v), count)
            far, near = moved // local, lax.rem(moved, local)
            g = [all_green[v // local, part, v % local] for part in range(2)]
            s = [all_single[v // local, part, v % local] for part in range(2)]
            gm = [all_green[far, part, near] for part in range(2)]
            sm = [all_single[far, part, near] for part in range(2)]
            first = times_complex(g[0], g[1], sm[0], sm[1])
            second = times_complex(s[0], s[1], gm[0], gm[1])
            real = real + (first[0] + second[0])
            imag = imag + (first[1] + second[1])
        for part, value in enumerate((real, imag)):
            bubble[part, w] = jnp.dot(value * factor, pick, precision=lax.Precision.HIGHEST,
                                      preferred_element_type=jnp.float32)

    def own(i):
        return pltpu.make_async_copy(send.at[i, b], land.at[i, b], own_sem.at[i])

    def outgoing(i, step):
        to = partner(b, step, nb)
        return pltpu.make_async_remote_copy(
            src_ref=send.at[i, to], dst_ref=land.at[i, b], send_sem=send_sem.at[i, step],
            recv_sem=recv_sem.at[i, step], device_id={"bond": to},
            device_id_type=pl.DeviceIdType.MESH)

    half_rows, half_count = order // 2, nb // 2

    def compute(i, carry):
        w, s = i // sites_here, lax.rem(i, sites_here)
        fetch(i).wait()
        gr, gi = gamma[i, 0], gamma[i, 1]
        br, bi = bubble[0, w, pl.ds(s, 1), :], bubble[1, w, pl.ds(s, 1), :]
        right_real = jnp.concatenate([gr, -gi], axis=0)
        right_imag = jnp.concatenate([gi, gr], axis=0)
        own_half = b // half_count
        for turn in range(2):
            half = lax.rem(own_half + 1 + turn, 2)
            top = pl.ds(pl.multiple_of(half * half_rows, half_rows), half_rows)
            grf, gif = gamma[i, 0, top, :].astype(jnp.float32), gamma[i, 1, top, :].astype(jnp.float32)
            lr = (grf * br - gif * bi).astype(jnp.bfloat16)
            li = (grf * bi + gif * br).astype(jnp.bfloat16)
            left = jnp.concatenate([lr, li], axis=1)
            for part, right in enumerate((right_real, right_imag)):
                flow = jnp.dot(left, right, preferred_element_type=jnp.float32)
                kept = (flow * masks[w, top, :]).astype(jnp.bfloat16)
                moved = jnp.dot(kept, shuffle[...], preferred_element_type=jnp.float32).astype(jnp.bfloat16)
                for d in range(half_count):
                    send[i, half * half_count + d, part] = moved[d * rows:(d + 1) * rows]
            if turn == 0:
                @pl.when(i >= WINDOW)
                def _():
                    receive(i - WINDOW)

                for step in range(nb - 1, half_count - 1, -1):
                    outgoing(i, step).start()
        for step in range(half_count - 1, 0, -1):
            outgoing(i, step).start()
        own(i).start()
        return carry

    def arrange(i, src):
        w, s = i // sites_here, lax.rem(i, sites_here)
        for part in range(2):
            block = land[i, src, part].astype(jnp.float32)
            for c in range(order // LANES):
                stage[w, part, c, pl.ds(src * sites_here + s, rows, stride=seg), :] = (
                    block[:, c * LANES:(c + 1) * LANES])

    def receive(i):
        own(i).wait()
        arrange(i, b)
        for step in range(1, nb):
            copy = outgoing(i, step)
            copy.wait_recv()
            arrange(i, origin(b, step, nb))

        @pl.when(lax.rem(i, sites_here) == sites_here - 1)
        def _():
            w = i // sites_here
            for part in range(2):
                for c in range(order // LANES):
                    out[part, w, :, :, c * LANES:(c + 1) * LANES] = (
                        stage[w, part, c].reshape(rows, seg, LANES).astype(jnp.bfloat16))

    def receive_last(i, carry):
        receive(i)
        return carry

    lax.fori_loop(0, items, compute, 0)
    lax.fori_loop(items - WINDOW, items, receive_last, 0)
    def drain(i, carry):
        for step in range(1, nb):
            outgoing(i, step).wait_send()
        return carry

    lax.fori_loop(0, items, drain, 0)


def body(nf, nb, gamma, green, single, bond_site, causal_mask, site_perm):
    _, local, sites_here, order, _ = gamma.shape
    sites = green.shape[-1]
    rows = order // nb
    seg = nb * sites_here
    items = local * sites_here
    result_bytes = 2 * local * rows * seg * order * 2
    vmem = pl.BlockSpec(memory_space=pltpu.VMEM)
    dma = pltpu.SemaphoreType.DMA
    return pl.pallas_call(
        functools.partial(kernel, nf, nb),
        out_shape=pltpu.VMEM((2, local, rows, seg, order), jnp.bfloat16),
        in_specs=[pl.BlockSpec(memory_space=pl.ANY), vmem, vmem, vmem, pl.BlockSpec(memory_space=pltpu.SMEM), vmem],
        out_specs=vmem,
        scratch_shapes=[
            pltpu.VMEM((items, 2, order, order), jnp.bfloat16),
            dma((items,)),
            pltpu.VMEM((nf, 2, local, sites_here, sites), jnp.float32),
            pltpu.VMEM((nf, 2, local, sites_here, sites), jnp.float32),
            pltpu.VMEM((2, local, sites_here, order), jnp.float32),
            pltpu.VMEM((local, order, order), jnp.float32),
            pltpu.VMEM((order, order), jnp.bfloat16),
            pltpu.VMEM((items, nb, 2, rows, order), jnp.bfloat16),
            pltpu.VMEM((items, nb, 2, rows, order), jnp.bfloat16),
            pltpu.VMEM((local, 2, order // LANES, rows * seg, LANES), jnp.float32),
            dma((nf,)), dma((nf,)), dma((nf,)), dma((nf,)),
            dma((items, nb)), dma((items, nb)), dma((items,)),
        ],
        compiler_params=pltpu.CompilerParams(
            collective_id=0, has_side_effects=True, vmem_limit_bytes=VMEM_BYTES - result_bytes),
        name="flow_exchange",
    )(gamma, green, single, bond_site, causal_mask.transpose(1, 0, 2), site_perm)


def solution(mesh):
    in_specs = (
        P(None, "freq", "bond", None, None),
        P(None, "freq", "bond", None),
        P(None, "freq", "bond", None),
        P(),
        P("freq", None, None),
        P(),
    )
    out_specs = P(None, "freq", "bond", None, None)
    run = functools.partial(body, mesh.shape["freq"], mesh.shape["bond"])
    return jax.shard_map(run, mesh=mesh, in_specs=in_specs, out_specs=out_specs, check_vma=False)
```

```python
import functools
import math

import jax
import jax.numpy as jnp
from jax import lax
from jax.experimental import pallas as pl
from jax.experimental.pallas import tpu as pltpu
from jax.sharding import PartitionSpec as P

LANES = 128
WINDOW = 2
VMEM_BYTES = 67_043_328


def partner(index, step, count):
    if count & (count - 1):
        return lax.rem(index + step, count)
    found = 0
    bit = 1
    while bit < count:
        found = found + lax.rem(index // bit + (step // bit) % 2, 2) * bit
        bit *= 2
    return found


def origin(index, step, count):
    if count & (count - 1):
        return lax.rem(index + count - step, count)
    return partner(index, step, count)


def times_complex(a, b, c, d):
    return a * c - b * d, a * d + b * c


def kernel(nf, nb, gamma_hbm, green, single, bond, mask, perm, out,
           gamma, gamma_sem, all_green, all_single, bubble, masks, shuffle, send, land, stage,
           recv_g, recv_s, send_g, send_s, send_sem, recv_sem, own_sem):
    _, local, sites_here, order, _ = gamma_hbm.shape
    sites = green.shape[-1]
    blocks = mask.shape[-1]
    width = order // blocks
    rows = order // nb
    count = local * nf
    seg = nb * sites_here
    items = local * sites_here
    f = lax.axis_index("freq")
    b = lax.axis_index("bond")

    def fetch(i):
        w, s = i // sites_here, lax.rem(i, sites_here)
        return pltpu.make_async_copy(gamma_hbm.at[:, w, s], gamma.at[i], gamma_sem.at[i])

    def fetch_start(i, carry):
        fetch(i).start()
        return carry

    barrier = pltpu.get_barrier_semaphore()
    for step in range(1, nf):
        pl.semaphore_signal(barrier, inc=1, device_id={"freq": lax.rem(f + step, nf)},
                            device_id_type=pl.DeviceIdType.MESH)
    for step in range(1, nb):
        pl.semaphore_signal(barrier, inc=1, device_id={"bond": partner(b, step, nb)},
                            device_id_type=pl.DeviceIdType.MESH)
    lax.fori_loop(0, items, fetch_start, 0)

    pick = (lax.broadcasted_iota(jnp.int32, (sites, order), 0) == bond[...][None, :]).astype(jnp.float32)
    shuffle[...] = (lax.broadcasted_iota(jnp.int32, (order, order), 0) == perm[...][None, :]).astype(
        jnp.float32).astype(jnp.bfloat16)
    for w in range(local):
        for i in range(blocks):
            for j in range(blocks):
                masks[w, i * width:(i + 1) * width, j * width:(j + 1) * width] = jnp.full(
                    (width, width), mask[i, w, j].astype(jnp.float32), jnp.float32)

    pl.semaphore_wait(barrier, nf - 1 + nb - 1)

    def greens(step):
        to = lax.rem(f + step, nf)
        pair = []
        for source, landing, ss, rs in ((green, all_green, send_g, recv_g),
                                        (single, all_single, send_s, recv_s)):
            pair.append(pltpu.make_async_remote_copy(
                src_ref=source, dst_ref=landing.at[f], send_sem=ss.at[step],
                recv_sem=rs.at[step], device_id={"freq": to},
                device_id_type=pl.DeviceIdType.MESH))
        return pair

    for step in range(1, nf):
        for copy in greens(step):
            copy.start()
    all_green[f] = green[...]
    all_single[f] = single[...]

    for step in range(1, nf):
        for copy in greens(step):
            copy.wait()

    factor = 1.0 / math.sqrt(count)
    for w in range(local):
        real = jnp.zeros((sites_here, sites), jnp.float32)
        imag = jnp.zeros((sites_here, sites), jnp.float32)
        for v in range(count):
            moved = lax.rem(f * local + (w + v), count)
            far, near = moved // local, lax.rem(moved, local)
            g = [all_green[v // local, part, v % local] for part in range(2)]
            s = [all_single[v // local, part, v % local] for part in range(2)]
            gm = [all_green[far, part, near] for part in range(2)]
            sm = [all_single[far, part, near] for part in range(2)]
            first = times_complex(g[0], g[1], sm[0], sm[1])
            second = times_complex(s[0], s[1], gm[0], gm[1])
            real = real + (first[0] + second[0])
            imag = imag + (first[1] + second[1])
        for part, value in enumerate((real, imag)):
            bubble[part, w] = jnp.dot(value * factor, pick, precision=lax.Precision.HIGHEST,
                                      preferred_element_type=jnp.float32)

    def own(i):
        return pltpu.make_async_copy(send.at[i, b], land.at[i, b], own_sem.at[i])

    def outgoing(i, step):
        to = partner(b, step, nb)
        return pltpu.make_async_remote_copy(
            src_ref=send.at[i, to], dst_ref=land.at[i, b], send_sem=send_sem.at[i, step],
            recv_sem=recv_sem.at[i, step], device_id={"bond": to},
            device_id_type=pl.DeviceIdType.MESH)

    half_rows, half_count = order // 2, nb // 2

    def send_steps(i, high, low):
        for step in range(high, low, -1):
            outgoing(i, step).start()

    def compute(i, carry):
        w, s = i // sites_here, lax.rem(i, sites_here)
        fetch(i).wait()
        gr, gi = gamma[i, 0], gamma[i, 1]
        br, bi = bubble[0, w, pl.ds(s, 1), :], bubble[1, w, pl.ds(s, 1), :]
        right_real = jnp.concatenate([gr, -gi], axis=0)
        right_imag = jnp.concatenate([gi, gr], axis=0)
        own_half = b // half_count
        for turn in range(2):
            half = lax.rem(own_half + 1 + turn, 2)
            top = pl.ds(pl.multiple_of(half * half_rows, half_rows), half_rows)
            grf, gif = gamma[i, 0, top, :].astype(jnp.float32), gamma[i, 1, top, :].astype(jnp.float32)
            lr = (grf * br - gif * bi).astype(jnp.bfloat16)
            li = (grf * bi + gif * br).astype(jnp.bfloat16)
            left = jnp.concatenate([lr, li], axis=1)
            for part, right in enumerate((right_real, right_imag)):
                flow = jnp.dot(left, right, preferred_element_type=jnp.float32)
                kept = (flow * masks[w, top, :]).astype(jnp.bfloat16)
                moved = jnp.dot(kept, shuffle[...], preferred_element_type=jnp.float32).astype(jnp.bfloat16)
                for d in range(half_count):
                    send[i, half * half_count + d, part] = moved[d * rows:(d + 1) * rows]
            if turn == 0:
                @pl.when(i == 0)
                def _():
                    send_steps(i, nb - 1, half_count - 1)

        @pl.when(i >= WINDOW)
        def _():
            receive(i - WINDOW)

        send_steps(i, half_count - 1, 0)

        @pl.when(i > 0)
        def _():
            send_steps(i, nb - 1, half_count - 1)

        own(i).start()
        return carry

    def arrange(i, src):
        w, s = i // sites_here, lax.rem(i, sites_here)
        for part in range(2):
            block = land[i, src, part].astype(jnp.float32)
            for c in range(order // LANES):
                stage[w, part, c, pl.ds(src * sites_here + s, rows, stride=seg), :] = (
                    block[:, c * LANES:(c + 1) * LANES])

    def receive(i):
        own(i).wait()
        arrange(i, b)
        for step in range(1, nb):
            copy = outgoing(i, step)
            copy.wait_recv()
            arrange(i, origin(b, step, nb))

        @pl.when(lax.rem(i, sites_here) == sites_here - 1)
        def _():
            w = i // sites_here
            for part in range(2):
                for c in range(order // LANES):
                    out[part, w, :, :, c * LANES:(c + 1) * LANES] = (
                        stage[w, part, c].reshape(rows, seg, LANES).astype(jnp.bfloat16))

    def receive_last(i, carry):
        receive(i)
        return carry

    lax.fori_loop(0, items, compute, 0)
    lax.fori_loop(items - WINDOW, items, receive_last, 0)
    def drain(i, carry):
        for step in range(1, nb):
            outgoing(i, step).wait_send()
        return carry

    lax.fori_loop(0, items, drain, 0)


def body(nf, nb, gamma, green, single, bond_site, causal_mask, site_perm):
    _, local, sites_here, order, _ = gamma.shape
    sites = green.shape[-1]
    rows = order // nb
    seg = nb * sites_here
    items = local * sites_here
    result_bytes = 2 * local * rows * seg * order * 2
    vmem = pl.BlockSpec(memory_space=pltpu.VMEM)
    dma = pltpu.SemaphoreType.DMA
    return pl.pallas_call(
        functools.partial(kernel, nf, nb),
        out_shape=pltpu.VMEM((2, local, rows, seg, order), jnp.bfloat16),
        in_specs=[pl.BlockSpec(memory_space=pl.ANY), vmem, vmem, vmem, pl.BlockSpec(memory_space=pltpu.SMEM), vmem],
        out_specs=vmem,
        scratch_shapes=[
            pltpu.VMEM((items, 2, order, order), jnp.bfloat16),
            dma((items,)),
            pltpu.VMEM((nf, 2, local, sites_here, sites), jnp.float32),
            pltpu.VMEM((nf, 2, local, sites_here, sites), jnp.float32),
            pltpu.VMEM((2, local, sites_here, order), jnp.float32),
            pltpu.VMEM((local, order, order), jnp.float32),
            pltpu.VMEM((order, order), jnp.bfloat16),
            pltpu.VMEM((items, nb, 2, rows, order), jnp.bfloat16),
            pltpu.VMEM((items, nb, 2, rows, order), jnp.bfloat16),
            pltpu.VMEM((local, 2, order // LANES, rows * seg, LANES), jnp.float32),
            dma((nf,)), dma((nf,)), dma((nf,)), dma((nf,)),
            dma((items, nb)), dma((items, nb)), dma((items,)),
        ],
        compiler_params=pltpu.CompilerParams(
            collective_id=0, has_side_effects=True, vmem_limit_bytes=VMEM_BYTES - result_bytes),
        name="flow_exchange",
    )(gamma, green, single, bond_site, causal_mask.transpose(1, 0, 2), site_perm)


def solution(mesh):
    in_specs = (
        P(None, "freq", "bond", None, None),
        P(None, "freq", "bond", None),
        P(None, "freq", "bond", None),
        P(),
        P("freq", None, None),
        P(),
    )
    out_specs = P(None, "freq", "bond", None, None)
    run = functools.partial(body, mesh.shape["freq"], mesh.shape["bond"])
    return jax.shard_map(run, mesh=mesh, in_specs=in_specs, out_specs=out_specs, check_vma=False)
```

```python
import functools
import math

import jax
import jax.numpy as jnp
from jax import lax
from jax.experimental import pallas as pl
from jax.experimental.pallas import tpu as pltpu
from jax.sharding import PartitionSpec as P

LANES = 128
WINDOW = 2
VMEM_BYTES = 67_043_328


def partner(index, step, count):
    if count & (count - 1):
        return lax.rem(index + step, count)
    found = 0
    bit = 1
    while bit < count:
        found = found + lax.rem(index // bit + (step // bit) % 2, 2) * bit
        bit *= 2
    return found


def origin(index, step, count):
    if count & (count - 1):
        return lax.rem(index + count - step, count)
    return partner(index, step, count)


def times_complex(a, b, c, d):
    return a * c - b * d, a * d + b * c


def kernel(nf, nb, gamma_hbm, green, single, bond_hbm, mask_hbm, perm_hbm, out,
           gamma, gamma_sem, bond, mask, perm, values, small_sem, all_green, all_single, bubble, masks, shuffle, send, land, stage,
           recv_g, recv_s, send_g, send_s, send_sem, recv_sem, own_sem):
    _, local, sites_here, order, _ = gamma_hbm.shape
    sites = green.shape[-1]
    blocks = mask_hbm.shape[-1]
    width = order // blocks
    rows = order // nb
    count = local * nf
    seg = nb * sites_here
    items = local * sites_here
    f = lax.axis_index("freq")
    b = lax.axis_index("bond")

    def fetch(i):
        w, s = i // sites_here, lax.rem(i, sites_here)
        return pltpu.make_async_copy(gamma_hbm.at[:, w, s], gamma.at[i], gamma_sem.at[i])

    def fetch_start(i, carry):
        fetch(i).start()
        return carry

    barrier = pltpu.get_barrier_semaphore()
    for step in range(1, nf):
        pl.semaphore_signal(barrier, inc=1, device_id={"freq": lax.rem(f + step, nf)},
                            device_id_type=pl.DeviceIdType.MESH)
    for step in range(1, nb):
        pl.semaphore_signal(barrier, inc=1, device_id={"bond": partner(b, step, nb)},
                            device_id_type=pl.DeviceIdType.MESH)
    small = [
        pltpu.make_async_copy(source, kept, small_sem.at[k])
        for k, (source, kept) in enumerate((
            (bond_hbm, bond), (perm_hbm, perm), (mask_hbm, mask),
            (green, all_green.at[f]), (single, all_single.at[f])))
    ]
    for copy in small:
        copy.start()
    lax.fori_loop(0, items, fetch_start, 0)
    for copy in small:
        copy.wait()

    pick = (lax.broadcasted_iota(jnp.int32, (sites, order), 0) == bond[...][None, :]).astype(
        jnp.float32).astype(jnp.bfloat16)
    shuffle[...] = (lax.broadcasted_iota(jnp.int32, (order, order), 0) == perm[...][None, :]).astype(
        jnp.float32).astype(jnp.bfloat16)
    for w in range(local):
        for i in range(blocks):
            for j in range(blocks):
                masks[w, i * width:(i + 1) * width, j * width:(j + 1) * width] = jnp.full(
                    (width, width), mask[i, w, j].astype(jnp.float32), jnp.float32)

    pl.semaphore_wait(barrier, nf - 1 + nb - 1)

    def greens(step):
        to = lax.rem(f + step, nf)
        pair = []
        for source, landing, ss, rs in ((green, all_green, send_g, recv_g),
                                        (single, all_single, send_s, recv_s)):
            pair.append(pltpu.make_async_remote_copy(
                src_ref=source, dst_ref=landing.at[f], send_sem=ss.at[step],
                recv_sem=rs.at[step], device_id={"freq": to},
                device_id_type=pl.DeviceIdType.MESH))
        return pair

    for step in range(1, nf):
        for copy in greens(step):
            copy.start()

    for step in range(1, nf):
        for copy in greens(step):
            copy.wait()

    factor = 1.0 / math.sqrt(count)
    for w in range(local):
        real = jnp.zeros((sites_here, sites), jnp.float32)
        imag = jnp.zeros((sites_here, sites), jnp.float32)
        for v in range(count):
            moved = lax.rem(f * local + (w + v), count)
            far, near = moved // local, lax.rem(moved, local)
            g = [all_green[v // local, part, v % local] for part in range(2)]
            s = [all_single[v // local, part, v % local] for part in range(2)]
            gm = [all_green[far, part, near] for part in range(2)]
            sm = [all_single[far, part, near] for part in range(2)]
            first = times_complex(g[0], g[1], sm[0], sm[1])
            second = times_complex(s[0], s[1], gm[0], gm[1])
            real = real + (first[0] + second[0])
            imag = imag + (first[1] + second[1])
        for part, value in enumerate((real, imag)):
            values[part * items + w * sites_here:part * items + (w + 1) * sites_here] = value * factor

    whole = values[...]
    high = whole.astype(jnp.bfloat16)
    rest = whole - high.astype(jnp.float32)
    middle = rest.astype(jnp.bfloat16)
    low = (rest - middle.astype(jnp.float32)).astype(jnp.bfloat16)
    spread = jnp.dot(jnp.concatenate([high, middle, low], axis=0), pick,
                     preferred_element_type=jnp.float32)
    total = 2 * items
    spread = (spread[2 * total:] + spread[total:2 * total]) + spread[:total]
    for part in range(2):
        for w in range(local):
            top = part * items + w * sites_here
            bubble[part, w] = spread[top:top + sites_here]

    def own(i):
        return pltpu.make_async_copy(send.at[i, b], land.at[i, b], own_sem.at[i])

    def outgoing(i, step):
        to = partner(b, step, nb)
        return pltpu.make_async_remote_copy(
            src_ref=send.at[i, to], dst_ref=land.at[i, b], send_sem=send_sem.at[i, step],
            recv_sem=recv_sem.at[i, step], device_id={"bond": to},
            device_id_type=pl.DeviceIdType.MESH)

    half_rows, half_count = order // 2, nb // 2

    def send_steps(i, high, low):
        for step in range(high, low, -1):
            outgoing(i, step).start()

    def compute(i, carry):
        w, s = i // sites_here, lax.rem(i, sites_here)
        fetch(i).wait()
        gr, gi = gamma[i, 0], gamma[i, 1]
        br, bi = bubble[0, w, pl.ds(s, 1), :], bubble[1, w, pl.ds(s, 1), :]
        right_real = jnp.concatenate([gr, -gi], axis=0)
        right_imag = jnp.concatenate([gi, gr], axis=0)
        own_half = b // half_count
        for turn in range(2):
            half = lax.rem(own_half + 1 + turn, 2)
            top = pl.ds(pl.multiple_of(half * half_rows, half_rows), half_rows)
            grf, gif = gamma[i, 0, top, :].astype(jnp.float32), gamma[i, 1, top, :].astype(jnp.float32)
            lr = (grf * br - gif * bi).astype(jnp.bfloat16)
            li = (grf * bi + gif * br).astype(jnp.bfloat16)
            left = jnp.concatenate([lr, li], axis=1)
            for part, right in enumerate((right_real, right_imag)):
                flow = jnp.dot(left, right, preferred_element_type=jnp.float32)
                kept = (flow * masks[w, top, :]).astype(jnp.bfloat16)
                moved = jnp.dot(kept, shuffle[...], preferred_element_type=jnp.float32).astype(jnp.bfloat16)
                for d in range(half_count):
                    send[i, half * half_count + d, part] = moved[d * rows:(d + 1) * rows]
            if turn == 0:
                @pl.when(i == 0)
                def _():
                    send_steps(i, nb - 1, half_count - 1)

        @pl.when(i >= WINDOW)
        def _():
            receive(i - WINDOW)

        send_steps(i, half_count - 1, 0)

        @pl.when(i > 0)
        def _():
            send_steps(i, nb - 1, half_count - 1)

        own(i).start()
        return carry

    def arrange(i, src):
        w, s = i // sites_here, lax.rem(i, sites_here)
        for part in range(2):
            block = land[i, src, part].astype(jnp.float32)
            for c in range(order // LANES):
                stage[w, part, c, pl.ds(src * sites_here + s, rows, stride=seg), :] = (
                    block[:, c * LANES:(c + 1) * LANES])

    def receive(i):
        own(i).wait()
        arrange(i, b)
        for step in range(1, nb):
            copy = outgoing(i, step)
            copy.wait_recv()
            arrange(i, origin(b, step, nb))

        @pl.when(lax.rem(i, sites_here) == sites_here - 1)
        def _():
            w = i // sites_here
            for part in range(2):
                for c in range(order // LANES):
                    out[part, w, :, :, c * LANES:(c + 1) * LANES] = (
                        stage[w, part, c].reshape(rows, seg, LANES).astype(jnp.bfloat16))

    def receive_last(i, carry):
        receive(i)
        return carry

    lax.fori_loop(0, items, compute, 0)
    lax.fori_loop(items - WINDOW, items, receive_last, 0)
    def drain(i, carry):
        for step in range(1, nb):
            outgoing(i, step).wait_send()
        return carry

    lax.fori_loop(0, items, drain, 0)


def body(nf, nb, gamma, green, single, bond_site, causal_mask, site_perm):
    _, local, sites_here, order, _ = gamma.shape
    sites = green.shape[-1]
    blocks = causal_mask.shape[-1]
    rows = order // nb
    seg = nb * sites_here
    items = local * sites_here
    result_bytes = 2 * local * rows * seg * order * 2
    vmem = pl.BlockSpec(memory_space=pltpu.VMEM)
    dma = pltpu.SemaphoreType.DMA
    return pl.pallas_call(
        functools.partial(kernel, nf, nb),
        out_shape=pltpu.VMEM((2, local, rows, seg, order), jnp.bfloat16),
        in_specs=[pl.BlockSpec(memory_space=pl.ANY)] * 6,
        out_specs=vmem,
        scratch_shapes=[
            pltpu.VMEM((items, 2, order, order), jnp.bfloat16),
            dma((items,)),
            pltpu.VMEM((order,), jnp.int32),
            pltpu.SMEM((blocks, local, blocks), jnp.int32),
            pltpu.VMEM((order,), jnp.int32),
            pltpu.VMEM((2 * items, sites), jnp.float32),
            dma((5,)),
            pltpu.VMEM((nf, 2, local, sites_here, sites), jnp.float32),
            pltpu.VMEM((nf, 2, local, sites_here, sites), jnp.float32),
            pltpu.VMEM((2, local, sites_here, order), jnp.float32),
            pltpu.VMEM((local, order, order), jnp.float32),
            pltpu.VMEM((order, order), jnp.bfloat16),
            pltpu.VMEM((items, nb, 2, rows, order), jnp.bfloat16),
            pltpu.VMEM((items, nb, 2, rows, order), jnp.bfloat16),
            pltpu.VMEM((local, 2, order // LANES, rows * seg, LANES), jnp.float32),
            dma((nf,)), dma((nf,)), dma((nf,)), dma((nf,)),
            dma((items, nb)), dma((items, nb)), dma((items,)),
        ],
        compiler_params=pltpu.CompilerParams(
            collective_id=0, has_side_effects=True, vmem_limit_bytes=VMEM_BYTES - result_bytes),
        name="flow_exchange",
    )(gamma, green, single, bond_site, causal_mask.transpose(1, 0, 2), site_perm)


def solution(mesh):
    in_specs = (
        P(None, "freq", "bond", None, None),
        P(None, "freq", "bond", None),
        P(None, "freq", "bond", None),
        P(),
        P("freq", None, None),
        P(),
    )
    out_specs = P(None, "freq", "bond", None, None)
    run = functools.partial(body, mesh.shape["freq"], mesh.shape["bond"])
    return jax.shard_map(run, mesh=mesh, in_specs=in_specs, out_specs=out_specs, check_vma=False)
```

```python
import functools
import math

import jax
import jax.numpy as jnp
from jax import lax
from jax.experimental import pallas as pl
from jax.experimental.pallas import tpu as pltpu
from jax.sharding import PartitionSpec as P

LANES = 128
WINDOW = 2
VMEM_BYTES = 67_043_328


def partner(index, step, count):
    if count & (count - 1):
        return lax.rem(index + step, count)
    found = 0
    bit = 1
    while bit < count:
        found = found + lax.rem(index // bit + (step // bit) % 2, 2) * bit
        bit *= 2
    return found


def origin(index, step, count):
    if count & (count - 1):
        return lax.rem(index + count - step, count)
    return partner(index, step, count)


def times_complex(a, b, c, d):
    return a * c - b * d, a * d + b * c


def kernel(nf, nb, gamma_hbm, green, single, bond_hbm, mask_hbm, perm_hbm, out,
           gamma, gamma_sem, bond, mask, perm, values, small_sem, all_green, all_single, bubble, masks, shuffle, send, land, stage,
           recv_g, recv_s, send_g, send_s, send_sem, recv_sem, own_sem):
    _, local, sites_here, order, _ = gamma_hbm.shape
    sites = green.shape[-1]
    blocks = mask_hbm.shape[-1]
    width = order // blocks
    rows = order // nb
    count = local * nf
    seg = nb * sites_here
    items = local * sites_here
    groups, deep = stage.shape[3], seg // stage.shape[3]
    per = nb // groups
    f = lax.axis_index("freq")
    b = lax.axis_index("bond")

    def fetch(i):
        w, s = i // sites_here, lax.rem(i, sites_here)
        return pltpu.make_async_copy(gamma_hbm.at[:, w, s], gamma.at[i], gamma_sem.at[i])

    def fetch_start(i, carry):
        fetch(i).start()
        return carry

    barrier = pltpu.get_barrier_semaphore()
    for step in range(1, nf):
        pl.semaphore_signal(barrier, inc=1, device_id={"freq": lax.rem(f + step, nf)},
                            device_id_type=pl.DeviceIdType.MESH)
    for step in range(1, nb):
        pl.semaphore_signal(barrier, inc=1, device_id={"bond": partner(b, step, nb)},
                            device_id_type=pl.DeviceIdType.MESH)
    small = [
        pltpu.make_async_copy(source, kept, small_sem.at[k])
        for k, (source, kept) in enumerate((
            (bond_hbm, bond), (perm_hbm, perm), (mask_hbm, mask),
            (green, all_green.at[f]), (single, all_single.at[f])))
    ]
    for copy in small:
        copy.start()
    lax.fori_loop(0, items, fetch_start, 0)
    for copy in small:
        copy.wait()

    pick = (lax.broadcasted_iota(jnp.int32, (sites, order), 0) == bond[...][None, :]).astype(
        jnp.float32).astype(jnp.bfloat16)
    shuffle[...] = (lax.broadcasted_iota(jnp.int32, (order, order), 0) == perm[...][None, :]).astype(
        jnp.float32).astype(jnp.bfloat16)
    for w in range(local):
        for i in range(blocks):
            for j in range(blocks):
                masks[w, i * width:(i + 1) * width, j * width:(j + 1) * width] = jnp.full(
                    (width, width), mask[i, w, j].astype(jnp.float32), jnp.float32)

    pl.semaphore_wait(barrier, nf - 1 + nb - 1)

    def greens(step):
        to = lax.rem(f + step, nf)
        pair = []
        for source, landing, ss, rs in ((green, all_green, send_g, recv_g),
                                        (single, all_single, send_s, recv_s)):
            pair.append(pltpu.make_async_remote_copy(
                src_ref=source, dst_ref=landing.at[f], send_sem=ss.at[step],
                recv_sem=rs.at[step], device_id={"freq": to},
                device_id_type=pl.DeviceIdType.MESH))
        return pair

    for step in range(1, nf):
        for copy in greens(step):
            copy.start()

    for step in range(1, nf):
        for copy in greens(step):
            copy.wait()

    factor = 1.0 / math.sqrt(count)
    for w in range(local):
        real = jnp.zeros((sites_here, sites), jnp.float32)
        imag = jnp.zeros((sites_here, sites), jnp.float32)
        for v in range(count):
            moved = lax.rem(f * local + (w + v), count)
            far, near = moved // local, lax.rem(moved, local)
            g = [all_green[v // local, part, v % local] for part in range(2)]
            s = [all_single[v // local, part, v % local] for part in range(2)]
            gm = [all_green[far, part, near] for part in range(2)]
            sm = [all_single[far, part, near] for part in range(2)]
            first = times_complex(g[0], g[1], sm[0], sm[1])
            second = times_complex(s[0], s[1], gm[0], gm[1])
            real = real + (first[0] + second[0])
            imag = imag + (first[1] + second[1])
        for part, value in enumerate((real, imag)):
            values[part * items + w * sites_here:part * items + (w + 1) * sites_here] = value * factor

    whole = values[...]
    high = whole.astype(jnp.bfloat16)
    rest = whole - high.astype(jnp.float32)
    middle = rest.astype(jnp.bfloat16)
    low = (rest - middle.astype(jnp.float32)).astype(jnp.bfloat16)
    spread = jnp.dot(jnp.concatenate([high, middle, low], axis=0), pick,
                     preferred_element_type=jnp.float32)
    total = 2 * items
    spread = (spread[2 * total:] + spread[total:2 * total]) + spread[:total]
    for part in range(2):
        for w in range(local):
            top = part * items + w * sites_here
            bubble[part, w] = spread[top:top + sites_here]

    def own(i):
        return pltpu.make_async_copy(send.at[i, b], land.at[i, b], own_sem.at[i])

    def outgoing(i, step):
        to = partner(b, step, nb)
        return pltpu.make_async_remote_copy(
            src_ref=send.at[i, to], dst_ref=land.at[i, b], send_sem=send_sem.at[i, step],
            recv_sem=recv_sem.at[i, step], device_id={"bond": to},
            device_id_type=pl.DeviceIdType.MESH)

    half_rows, half_count = order // 2, nb // 2

    def send_steps(i, high, low):
        for step in range(high, low, -1):
            outgoing(i, step).start()

    def compute(i, carry):
        w, s = i // sites_here, lax.rem(i, sites_here)
        fetch(i).wait()
        gr, gi = gamma[i, 0], gamma[i, 1]
        br, bi = bubble[0, w, pl.ds(s, 1), :], bubble[1, w, pl.ds(s, 1), :]
        right_real = jnp.concatenate([gr, -gi], axis=0)
        right_imag = jnp.concatenate([gi, gr], axis=0)
        own_half = b // half_count
        for turn in range(2):
            half = lax.rem(own_half + 1 + turn, 2)
            top = pl.ds(pl.multiple_of(half * half_rows, half_rows), half_rows)
            grf, gif = gamma[i, 0, top, :].astype(jnp.float32), gamma[i, 1, top, :].astype(jnp.float32)
            lr = (grf * br - gif * bi).astype(jnp.bfloat16)
            li = (grf * bi + gif * br).astype(jnp.bfloat16)
            left = jnp.concatenate([lr, li], axis=1)
            for part, right in enumerate((right_real, right_imag)):
                flow = jnp.dot(left, right, preferred_element_type=jnp.float32)
                kept = (flow * masks[w, top, :]).astype(jnp.bfloat16)
                moved = jnp.dot(kept, shuffle[...], preferred_element_type=jnp.float32).astype(jnp.bfloat16)
                for d in range(half_count):
                    send[i, half * half_count + d, part] = moved[d * rows:(d + 1) * rows]
            if turn == 0:
                @pl.when(i == 0)
                def _():
                    send_steps(i, nb - 1, half_count - 1)

        @pl.when(i >= WINDOW)
        def _():
            receive(i - WINDOW)

        send_steps(i, half_count - 1, 0)

        @pl.when(i > 0)
        def _():
            send_steps(i, nb - 1, half_count - 1)

        own(i).start()
        return carry

    def arrange(i, src):
        w, s = i // sites_here, lax.rem(i, sites_here)
        for part in range(2):
            block = land[i, src, part].astype(jnp.float32)
            for c in range(order // LANES):
                stage[w, part, c, src // per, pl.ds(lax.rem(src, per) * sites_here + s, rows, stride=deep), :] = (
                    block[:, c * LANES:(c + 1) * LANES])

    def finish(i, group):
        @pl.when(lax.rem(i, sites_here) == sites_here - 1)
        def _():
            w = i // sites_here
            place = pl.ds(pl.multiple_of(group * deep, deep), deep)
            for part in range(2):
                for c in range(order // LANES):
                    out[part, w, :, place, c * LANES:(c + 1) * LANES] = (
                        stage[w, part, c, group].reshape(rows, deep, LANES).astype(jnp.bfloat16))

    def receive(i):
        own(i).wait()
        arrange(i, b)
        for step in range(1, nb):
            copy = outgoing(i, step)
            copy.wait_recv()
            arrange(i, origin(b, step, nb))
            if (step + 1) % per == 0:
                finish(i, origin(b, step, nb) // per)

    def receive_last(i, carry):
        receive(i)
        return carry

    lax.fori_loop(0, items, compute, 0)
    lax.fori_loop(items - WINDOW, items, receive_last, 0)
    def drain(i, carry):
        for step in range(1, nb):
            outgoing(i, step).wait_send()
        return carry

    lax.fori_loop(0, items, drain, 0)


def body(nf, nb, gamma, green, single, bond_site, causal_mask, site_perm):
    _, local, sites_here, order, _ = gamma.shape
    sites = green.shape[-1]
    blocks = causal_mask.shape[-1]
    rows = order // nb
    seg = nb * sites_here
    items = local * sites_here
    deep = 8 if sites_here < 8 else sites_here
    result_bytes = 2 * local * rows * seg * order * 2
    vmem = pl.BlockSpec(memory_space=pltpu.VMEM)
    dma = pltpu.SemaphoreType.DMA
    return pl.pallas_call(
        functools.partial(kernel, nf, nb),
        out_shape=pltpu.VMEM((2, local, rows, seg, order), jnp.bfloat16),
        in_specs=[pl.BlockSpec(memory_space=pl.ANY)] * 6,
        out_specs=vmem,
        scratch_shapes=[
            pltpu.VMEM((items, 2, order, order), jnp.bfloat16),
            dma((items,)),
            pltpu.VMEM((order,), jnp.int32),
            pltpu.SMEM((blocks, local, blocks), jnp.int32),
            pltpu.VMEM((order,), jnp.int32),
            pltpu.VMEM((2 * items, sites), jnp.float32),
            dma((5,)),
            pltpu.VMEM((nf, 2, local, sites_here, sites), jnp.float32),
            pltpu.VMEM((nf, 2, local, sites_here, sites), jnp.float32),
            pltpu.VMEM((2, local, sites_here, order), jnp.float32),
            pltpu.VMEM((local, order, order), jnp.float32),
            pltpu.VMEM((order, order), jnp.bfloat16),
            pltpu.VMEM((items, nb, 2, rows, order), jnp.bfloat16),
            pltpu.VMEM((items, nb, 2, rows, order), jnp.bfloat16),
            pltpu.VMEM((local, 2, order // LANES, seg // deep, rows * deep, LANES), jnp.float32),
            dma((nf,)), dma((nf,)), dma((nf,)), dma((nf,)),
            dma((items, nb)), dma((items, nb)), dma((items,)),
        ],
        compiler_params=pltpu.CompilerParams(
            collective_id=0, has_side_effects=True, vmem_limit_bytes=VMEM_BYTES - result_bytes),
        name="flow_exchange",
    )(gamma, green, single, bond_site, causal_mask.transpose(1, 0, 2), site_perm)


def solution(mesh):
    in_specs = (
        P(None, "freq", "bond", None, None),
        P(None, "freq", "bond", None),
        P(None, "freq", "bond", None),
        P(),
        P("freq", None, None),
        P(),
    )
    out_specs = P(None, "freq", "bond", None, None)
    run = functools.partial(body, mesh.shape["freq"], mesh.shape["bond"])
    return jax.shard_map(run, mesh=mesh, in_specs=in_specs, out_specs=out_specs, check_vma=False)
```
